32 devices in a mesh: group: 2 (over y), dp: 4 (over x, core), seq: 4 (over z).
Axes of the slice: x: 2, y: 2, z: 4, core: 2. Of those that a mesh axis runs over, the one named last changes fastest.
Arguments:
- tokens: bfloat16 [8, 1024, 4096], P(('group', 'dp'), 'seq'), parts along dimension 0, may hold values from -6 to 6
- norm_gain: bfloat16 [4096], replicated, may hold values from 0.099609375 to 1.8984375
- qkv_weight: bfloat16 [4096, 3072], P('dp'), may hold values from -4 to 4, as said below
- doc_ids: int32 [8, 1024], P(('group', 'dp'), 'seq'), parts along dimension 0, may hold values from 0 to 5, never falling along the last dimension, each value on 1 to 512 neighbouring positions
Outputs:
- attended: bfloat16 [8, 1024, 2048], P(('group', 'dp'), 'seq'), parts along dimension 0
The draws below stay inside these ranges and needn't reach their ends.
There are 2 independent parts, one for each index of `group`. The reference program is written for one: setup_inputs(seed, part) draws one part's arguments, and reference() takes and returns one part's arrays. A program takes and returns all parts, laid end to end along the dimension named above; an argument that names none is the same for every part. Nothing has to cross between parts.
Inputs may be any that keep to these rules, and one draw needn't show every extreme that they name: `qkv_weight`: in the hidden draw query heads lie close to multiples of their key head. `doc_ids`: ids never fall along a sequence; a document holds at most 512 positions.
All inputs are finite; a program needn't handle non-finite values.
Results may differ from the reference program's by a relative error of at most 0.0075.
Values may be sent and summed in bfloat16 or wider, within the bound.
No kernel may reach another device: no remote copies, remote signals or barrier semaphores. Data moves between devices by JAX's collectives and lax.ppermute only.
A program may use at most 128 MiB of HBM per device.

```python
import math
import jax
import jax.numpy as jnp
import numpy as np
from jax import lax

D = 4096
HD = 128
QH = 16
KVH = 4
LEN = 1024
SEQS = 4
QW = 2048
KW = 512


def draw_qkv_weight(key, part):
    base = jnp.clip(jax.random.normal(key, (D, QW + 2 * KW), jnp.float32), -6.0, 6.0) / math.sqrt(D)
    return jnp.clip(base, -4.0, 4.0).astype(jnp.bfloat16)


def block_levels(stream_key, extent, pieces, low, top_value):
    def one(position, blocks):
        draws = jax.random.uniform(jax.random.fold_in(jax.random.fold_in(stream_key, 6), position), (blocks,), jnp.float32, low / len(pieces), top_value / len(pieces))
        return jnp.repeat(jnp.exp(draws), extent[position] // blocks).reshape((-1,) + (1,) * (len(extent) - position - 1))

    factor_of = one(*pieces[0])
    for cut in pieces[1:]:
        factor_of = factor_of * one(*cut)
    return factor_of


def profile(number_of, total, most, slope):
    portions = [(1 << 20) // math.isqrt(grade ** slope) + 1 for grade in range(2, number_of + 1)]
    rest, counts = total - most - (number_of - 1), [1] * (number_of - 1)
    while rest > 0:
        free = [i for i in range(number_of - 1) if counts[i] < most]
        pool, remaining = sum([portions[i] for i in free]), rest
        for i in free:
            more = min(most - counts[i], max(1, remaining * portions[i] // pool), rest)
            counts[i] = counts[i] + more
            rest = rest - more
    return np.array([most] + counts)


def uneven_parts(key, number_of, total, bound, lean):
    if number_of == 2:
        one = jax.random.randint(key, (), max(1, total - bound), min(bound, total - 1) + 1)
        return jnp.stack([one, total - one])
    tallies = jnp.asarray(profile(number_of, total, bound, lean), jnp.int32)
    pairs = (number_of - 1) // 2
    giver, receiver = tallies[1:1 + 2 * pairs:2], tallies[2:2 + 2 * pairs:2]
    room = jnp.minimum(giver - 1, bound - receiver)
    moved = jax.random.randint(jax.random.fold_in(key, 1), (pairs,), 0, 1 << 20) % (room + 1)
    tallies = tallies.at[1:1 + 2 * pairs:2].set(giver - moved).at[2:2 + 2 * pairs:2].set(receiver + moved)
    return tallies[jax.random.permutation(jax.random.fold_in(key, 2), number_of)]


def bell_draw(key, shape, deviation, reach, split=(), kind=jnp.bfloat16):
    values = deviation * jax.random.normal(key, shape, jnp.float32)
    if split:
        values = values * block_levels(key, shape, split, -0.22, 0.18)
    return jnp.clip(values, -reach, reach).astype(kind)


def setup_inputs(seed: int = 0, part: int = 0) -> dict:
    arg_keys = jax.random.split(jax.random.key(seed), 5)
    part_keys = jax.random.split(jax.random.fold_in(arg_keys[4], part), 5)
    return {
        "tokens": bell_draw(part_keys[0], (SEQS, LEN, D), 1.0, 6.0, ((0, 4), (1, 4))),
        "norm_gain": jnp.clip(1.0 + 0.18 * jax.random.normal(arg_keys[1], (D,), jnp.float32), 0.099609375, 1.8984375).astype(jnp.bfloat16),
        "qkv_weight": draw_qkv_weight(jax.random.fold_in(arg_keys[4], 71), part),
        "doc_ids": jax.vmap(lambda own: jnp.searchsorted(jnp.cumsum(uneven_parts(own, 6, LEN, LEN // 2, 1)), jnp.arange(LEN), side="right"))(jax.random.split(part_keys[3], SEQS)).reshape((SEQS, LEN)).astype(jnp.int32),
    }


def rms_norm(rows, gain):
    values = rows.astype(jnp.float32)
    scale = lax.rsqrt(lax.optimization_barrier(jnp.mean(values * values, axis=-1, keepdims=True)) + 1e-05)
    return (values * scale * gain.astype(jnp.float32)).astype(jnp.bfloat16)

def rotate(heads, places):
    half = heads.shape[-1] // 2
    freqs = 500000.0 ** (-2.0 * jnp.arange(half, dtype=jnp.float32) / heads.shape[-1])
    angles = places[:, None] * freqs[None, :]
    cosine = jnp.cos(angles)[:, None, :]
    sine = jnp.sin(angles)[:, None, :]
    first = heads[..., :half]
    second = heads[..., half:]
    return jnp.concatenate([first * cosine - second * sine, second * cosine + first * sine], axis=-1)

def one_sequence(rows, docs, gain, weight):
    normed = rms_norm(rows, gain)
    proj = jnp.dot(normed, weight, preferred_element_type=jnp.float32)
    places = jnp.arange(LEN, dtype=jnp.float32)
    queries = rotate(proj[:, :QW].reshape(LEN, QH, HD), places).astype(jnp.bfloat16)
    keys = rotate(proj[:, QW:QW + KW].reshape(LEN, KVH, HD), places).astype(jnp.bfloat16)
    values = proj[:, QW + KW:].reshape(LEN, KVH, HD).astype(jnp.bfloat16)
    ratio = QH // KVH
    queries = queries.reshape(LEN, KVH, ratio, HD)
    block = min(512, LEN)
    scale = 1.0 / HD ** 0.5
    cols = jnp.arange(LEN, dtype=jnp.int32)

    def one_block(index):
        start = (index * block).astype(jnp.int32)
        qblock = lax.dynamic_slice_in_dim(queries, start, block, 0)
        scores = jnp.einsum('qkgd,tkd->kgqt', qblock.astype(jnp.float32), keys.astype(jnp.float32)) * scale
        rowpos = start + jnp.arange(block, dtype=jnp.int32)
        rowdoc = lax.dynamic_slice_in_dim(docs, start, block, 0)
        allow = (cols[None, :] <= rowpos[:, None]) & (docs[None, :] == rowdoc[:, None])
        scores = jnp.where(allow[None, None], scores, -1e+30)
        peak = lax.optimization_barrier(jnp.max(scores, axis=-1, keepdims=True))
        expo = jnp.where(allow[None, None], jnp.exp(scores - peak), 0.0)
        total = lax.optimization_barrier(jnp.sum(expo, axis=-1))
        weights = expo.astype(jnp.bfloat16)
        outs = jnp.einsum('kgqt,tkd->qkgd', weights.astype(jnp.float32), values.astype(jnp.float32))
        outs = outs / jnp.transpose(total, (2, 0, 1))[..., None]
        return outs.reshape(block, QW).astype(jnp.bfloat16)
    result = lax.map(one_block, jnp.arange(LEN // block, dtype=jnp.int32))
    return result.reshape(LEN, QW)

def reference(tokens, norm_gain, qkv_weight, doc_ids):

    def step(pair):
        return one_sequence(pair[0], pair[1], norm_gain, qkv_weight)
    return lax.map(step, (tokens, doc_ids))
```

```python
import functools
import math

import jax
import jax.numpy as jnp
from jax import lax
from jax.experimental import pallas as pl
from jax.experimental.pallas import tpu as pltpu
from jax.sharding import PartitionSpec as P

HD = 128
QH = 16
KVH = 4
QW = 2048
KW = 512
SHARE = QH // KVH
GW = SHARE * HD
Q_CHUNKS = 2
EXP2_SCALE = math.log2(math.e) / math.sqrt(HD)


def norm_kernel(order_ref, tok_ref, gain_ref, *out_refs):
    depth = out_refs[0].shape[1] // 2
    values = tok_ref[...].astype(jnp.float32)
    scale = lax.rsqrt(jnp.mean(values * values, axis=-1, keepdims=True) + 1e-05)
    for place, out_ref in enumerate(out_refs):
        for half in range(2):
            start = pl.multiple_of(order_ref[2 * place + half] * depth, 128)
            piece = tok_ref[:, pl.ds(start, depth)].astype(jnp.float32)
            gain = gain_ref[:, pl.ds(start, depth)].astype(jnp.float32)
            out_ref[:, half * depth : (half + 1) * depth] = (piece * scale * gain).astype(
                jnp.bfloat16
            )


def norm_blocks(rows, gain, order, depth):
    tok, width = rows.shape
    chips = order.shape[0] // 2
    step = min(64, tok)
    return pl.pallas_call(
        norm_kernel,
        out_shape=[jax.ShapeDtypeStruct((tok, 2 * depth), jnp.bfloat16)] * chips,
        grid_spec=pltpu.PrefetchScalarGridSpec(
            num_scalar_prefetch=1,
            grid=(tok // step,),
            in_specs=[
                pl.BlockSpec((step, width), lambda i, order: (i, 0)),
                pl.BlockSpec((1, width), lambda i, order: (0, 0)),
            ],
            out_specs=[pl.BlockSpec((step, 2 * depth), lambda i, order: (i, 0))] * chips,
        ),
        name="norm_blocks",
    )(order, rows, gain.reshape(1, width))


def part_kernel(rows_ref, near_ref, far_ref, out_ref):
    depth = near_ref.shape[0]
    total = jnp.dot(rows_ref[:, :depth], near_ref[...], preferred_element_type=jnp.float32)
    total += jnp.dot(rows_ref[:, depth:], far_ref[...], preferred_element_type=jnp.float32)
    out_ref[...] = total.astype(out_ref.dtype)


def part_product(rows, near, far, first, width, dtype, tile=512):
    tok = rows.shape[0]
    depth = near.shape[0]
    base = first // tile
    weight_spec = pl.BlockSpec((depth, tile), lambda i: (0, base + i))
    return pl.pallas_call(
        part_kernel,
        out_shape=jax.ShapeDtypeStruct((tok, width), dtype),
        grid=(width // tile,),
        in_specs=[pl.BlockSpec((tok, 2 * depth), lambda i: (0, 0)), weight_spec, weight_spec],
        out_specs=pl.BlockSpec((tok, tile), lambda i: (0, i)),
        name="part_product",
    )(rows, near, far)


def turn(head, cosine, sine):
    return head * cosine + pltpu.roll(head, HD // 2, 1) * sine


def kv_kernel(cos_ref, sin_ref, own_ref, *refs):
    *got_refs, out_ref = refs
    total = own_ref[...]
    for got_ref in got_refs:
        total += got_ref[...].astype(jnp.float32)
    for head in range(KVH):
        cut = slice(head * HD, (head + 1) * HD)
        out_ref[:, cut] = turn(total[:, cut], cos_ref[...], sin_ref[...]).astype(jnp.bfloat16)
    out_ref[:, KW:] = total[:, KW:].astype(jnp.bfloat16)


def finish_kv(own, got, cosine, sine):
    tok = own.shape[0]
    return pl.pallas_call(
        kv_kernel,
        out_shape=jax.ShapeDtypeStruct((tok, 2 * KW), jnp.bfloat16),
        grid=(1,),
        in_specs=[pl.BlockSpec((tok, HD), lambda i: (0, 0))] * 2
        + [pl.BlockSpec((tok, 2 * KW), lambda i: (0, QW // (2 * KW)))]
        + [pl.BlockSpec((tok, 2 * KW), lambda i: (0, 0))] * len(got),
        out_specs=pl.BlockSpec((tok, 2 * KW), lambda i: (0, 0)),
        name="finish_kv",
    )(cosine, sine, own, *got)


def attend_kernel(parts, blocks, cos_ref, sin_ref, bias_ref, own_ref, *refs):
    got_refs = refs[:parts]
    key_refs = refs[parts : parts + blocks]
    value_refs = refs[parts + blocks : parts + 2 * blocks]
    out_ref = refs[-1]
    keys = jnp.concatenate([ref[...] for ref in key_refs], axis=0)
    values = jnp.concatenate([ref[...] for ref in value_refs], axis=0)
    values = jnp.concatenate([values, jnp.ones_like(values)], axis=1)
    for head in range(SHARE):
        cut = slice(head * HD, (head + 1) * HD)
        query = own_ref[:, cut]
        for got_ref in got_refs:
            query += got_ref[:, cut].astype(jnp.float32)
        query = turn(query, cos_ref[...], sin_ref[...]).astype(jnp.bfloat16)
        scores = lax.dot_general(
            query, keys, (((1,), (1,)), ((), ())), preferred_element_type=jnp.float32
        )
        scores = scores + bias_ref[...]
        peak = jnp.max(scores, axis=-1, keepdims=True)
        expo = jnp.exp2((scores - peak) * EXP2_SCALE).astype(jnp.bfloat16)
        sums = jnp.dot(expo, values, preferred_element_type=jnp.float32)
        out_ref[:, cut] = (sums[:, :HD] / sums[:, HD:]).astype(jnp.bfloat16)


def attend(own, got, kv_blocks, bias, cosine, sine, first, previous):
    tok = own.shape[0]
    blocks = len(kv_blocks)
    heads = QW // Q_CHUNKS // GW
    base = first // GW
    kv_base = base
    whole = lambda i: (0, 0)
    key_spec = pl.BlockSpec((tok, HD), lambda i: (0, kv_base + i))
    value_spec = pl.BlockSpec((tok, HD), lambda i: (0, KVH + kv_base + i))
    in_specs = [
        pl.BlockSpec((tok, HD), whole),
        pl.BlockSpec((tok, HD), whole),
        pl.BlockSpec((tok, blocks * tok), whole),
        pl.BlockSpec((tok, GW), lambda i: (0, base + i)),
    ]
    in_specs += [pl.BlockSpec((tok, GW), lambda i: (0, i))] * len(got)
    in_specs += [key_spec] * blocks + [value_spec] * blocks
    operands = [cosine, sine, bias, own, *got, *kv_blocks, *kv_blocks]
    aliases = {}
    kernel = functools.partial(attend_kernel, len(got), blocks)
    if previous is not None:
        aliases = {len(operands): 0}
        operands.append(previous)
        in_specs.append(pl.BlockSpec(memory_space=pl.ANY))
    return pl.pallas_call(
        kernel,
        out_shape=jax.ShapeDtypeStruct((tok, QW), jnp.bfloat16),
        grid=(heads,),
        in_specs=in_specs,
        out_specs=pl.BlockSpec((tok, GW), lambda i: (0, base + i)),
        input_output_aliases=aliases,
        name="attend",
    )(*operands)


def local(tokens, norm_gain, qkv_weight, doc_ids):
    count = lax.axis_size("seq")
    rank = lax.axis_index("seq")
    ranks = lax.axis_size("dp")
    place = lax.axis_index("dp")
    chips = ranks // 2
    tok = tokens.shape[1]
    depth = qkv_weight.shape[0]
    hops = -(-(tok * count // 2 - 1) // tok)

    far = lax.ppermute(qkv_weight, "dp", [(i, i ^ 1) for i in range(ranks)])
    near = qkv_weight
    order = jnp.stack(
        [((place + 2 * j) % ranks) ^ half for j in range(chips) for half in range(2)]
    ).astype(jnp.int32)
    mine, *sent = norm_blocks(tokens[0], norm_gain, order, depth)
    guests = [
        lax.ppermute(part, "dp", [(i, (i + 2 * j) % ranks) for i in range(ranks)])
        for j, part in enumerate(sent, 1)
    ]

    half = HD // 2
    places = (rank * tok + jnp.arange(tok, dtype=jnp.int32)).astype(jnp.float32)
    freqs = 500000.0 ** (-2.0 * jnp.arange(half, dtype=jnp.float32) / HD)
    angles = places[:, None] * freqs[None, :]
    cosine = jnp.cos(angles)
    sine = jnp.sin(angles)
    cosine = jnp.concatenate([cosine, cosine], axis=1)
    sine = jnp.concatenate([-sine, sine], axis=1)

    docs = doc_ids[0]
    spots = jnp.arange(tok, dtype=jnp.int32)
    allow = [(spots[None, :] <= spots[:, None]) & (docs[None, :] == docs[:, None])]
    for hop in range(1, hops + 1):
        other = lax.ppermute(doc_ids, "seq", [(i, i + hop) for i in range(count - hop)])[0]
        allow.append((rank >= hop) & (other[None, :] == docs[:, None]))
    bias = jnp.where(jnp.concatenate(allow, axis=1), 0.0, -1e30).astype(jnp.float32)

    own = part_product(mine, near, far, 0, QW + 2 * KW, jnp.float32)

    def home(part, j):
        return lax.ppermute(part, "dp", [(i, (i - 2 * j) % ranks) for i in range(ranks)])

    kv_got = [
        home(part_product(rows, near, far, QW, 2 * KW, jnp.bfloat16), j)
        for j, rows in enumerate(guests, 1)
    ]
    q_step = QW // Q_CHUNKS
    q_got = [
        [
            home(part_product(rows, near, far, chunk * q_step, q_step, jnp.bfloat16), j)
            for j, rows in enumerate(guests, 1)
        ]
        for chunk in range(Q_CHUNKS)
    ]
    block = finish_kv(own, kv_got, cosine, sine)
    kv_blocks = [block]
    for hop in range(hops):
        block = lax.ppermute(block, "seq", [(i, i + 1) for i in range(count - 1)])
        kv_blocks.append(block)
    result = None
    for chunk in range(Q_CHUNKS):
        result = attend(
            own, q_got[chunk], kv_blocks, bias, cosine, sine, chunk * q_step, result
        )
    return result[None]


def solution(mesh):
    in_specs = (P(("group", "dp"), "seq", None), P(), P("dp", None), P(("group", "dp"), "seq"))
    out_specs = P(("group", "dp"), "seq", None)
    return jax.shard_map(local, mesh=mesh, in_specs=in_specs, out_specs=out_specs, check_vma=False)
```

```python
import functools
import math

import jax
import jax.numpy as jnp
from jax import lax
from jax.experimental import pallas as pl
from jax.experimental.pallas import tpu as pltpu
from jax.sharding import PartitionSpec as P


HD = 128
QH = 16
KVH = 4
QW = 2048
KW = 512
SHARE = QH // KVH
EXP2_SCALE = math.log2(math.e) / math.sqrt(HD)
HALVES = 2

ANY = pl.BlockSpec(memory_space=pl.ANY)


def row_scale(values):
    return lax.rsqrt(jnp.mean(values * values, axis=-1, keepdims=True) + 1e-05)


def write_blocks(tok_ref, gain_ref, scale, out_ref, chip, core):
    depth = out_ref.shape[1] // 2
    for half in range(2):
        block = 2 * chip + (core if half == 0 else 1 - core)
        cut = pl.ds(pl.multiple_of(block * depth, 128), depth)
        piece = tok_ref[:, cut].astype(jnp.float32) * scale
        piece = piece * gain_ref[cut].astype(jnp.float32)[None, :]
        out_ref[:, half * depth : (half + 1) * depth] = piece.astype(jnp.bfloat16)


def norm_kernel(chips, tok_ref, gain_ref, *out_refs):
    place = lax.axis_index("dp")
    scale = row_scale(tok_ref[...].astype(jnp.float32))
    for j, out_ref in enumerate(out_refs, 1):
        chip = lax.rem(lax.div(place, 2) + j, chips)
        write_blocks(tok_ref, gain_ref, scale, out_ref, chip, lax.rem(place, 2))


def norm_sent(rows, gain, part, depth, chips):
    tok, width = rows.shape
    step = tok // HALVES
    return pl.pallas_call(
        functools.partial(norm_kernel, chips),
        out_shape=[jax.ShapeDtypeStruct((step, 2 * depth), jnp.bfloat16)] * (chips - 1),
        grid=(1,),
        in_specs=[
            pl.BlockSpec((step, width), lambda i: (part, 0)),
            pl.BlockSpec((width,), lambda i: (0,)),
        ],
        out_specs=[pl.BlockSpec((step, 2 * depth), lambda i: (0, 0))] * (chips - 1),
        compiler_params=pltpu.CompilerParams(vmem_limit_bytes=64 * 1024 * 1024),
        name="norm_sent",
    )(rows, gain)


def weight_copies(first, width, tile, near_hbm, far_hbm, near, far, sems):
    copies = []
    for c in range(width // tile):
        cut = pl.ds(first + c * tile, tile)
        kept = pl.ds(c * tile, tile)
        copies.append(
            (
                pltpu.make_async_copy(near_hbm.at[:, cut], near.at[:, kept], sems.at[c, 0]),
                pltpu.make_async_copy(far_hbm.at[:, cut], far.at[:, kept], sems.at[c, 1]),
            )
        )
    for pair in copies:
        for copy in pair:
            copy.start()
    return copies


def multiply(rows, copies, tile, near, far, out_ref):
    depth = near.shape[0]
    for c, (near_copy, far_copy) in enumerate(copies):
        kept = slice(c * tile, (c + 1) * tile)
        near_copy.wait()
        total = jnp.dot(rows[:, :depth], near[:, kept], preferred_element_type=jnp.float32)
        far_copy.wait()
        total += jnp.dot(rows[:, depth:], far[:, kept], preferred_element_type=jnp.float32)
        out_ref[:, kept] = total.astype(out_ref.dtype)


def own_kernel(tile, tok_ref, gain_ref, near_hbm, far_hbm, out_ref, near, far, mine, sems):
    copies = weight_copies(0, out_ref.shape[1], tile, near_hbm, far_hbm, near, far, sems)
    place = lax.axis_index("dp")
    scale = row_scale(tok_ref[...].astype(jnp.float32))
    write_blocks(tok_ref, gain_ref, scale, mine, lax.div(place, 2), lax.rem(place, 2))
    multiply(mine, copies, tile, near, far, out_ref)


def own_product(rows, gain, near, far, tile=512):
    tok, width = rows.shape
    depth, columns = near.shape
    whole = lambda i: (0, 0)
    return pl.pallas_call(
        functools.partial(own_kernel, tile),
        out_shape=jax.ShapeDtypeStruct((tok, columns), jnp.float32),
        grid=(1,),
        in_specs=[pl.BlockSpec((tok, width), whole), pl.BlockSpec((width,), lambda i: (0,)), ANY, ANY],
        out_specs=pl.BlockSpec((tok, columns), whole),
        scratch_shapes=[
            pltpu.VMEM((depth, columns), jnp.bfloat16),
            pltpu.VMEM((depth, columns), jnp.bfloat16),
            pltpu.VMEM((tok, 2 * depth), jnp.bfloat16),
            pltpu.SemaphoreType.DMA((columns // tile, 2)),
        ],
        compiler_params=pltpu.CompilerParams(vmem_limit_bytes=64 * 1024 * 1024),
        name="own_product",
    )(rows, gain, near, far)


def guest_kernel(first, tile, rows_hbm, near_hbm, far_hbm, out_ref, rows, near, far, sems, sem):
    rows_copy = pltpu.make_async_copy(rows_hbm, rows, sem)
    rows_copy.start()
    copies = weight_copies(first, out_ref.shape[1], tile, near_hbm, far_hbm, near, far, sems)
    rows_copy.wait()
    multiply(rows, copies, tile, near, far, out_ref)


def guest_product(rows, near, far, first, width, tile=512):
    tok = rows.shape[0]
    depth = near.shape[0]
    return pl.pallas_call(
        functools.partial(guest_kernel, first, tile),
        out_shape=jax.ShapeDtypeStruct((tok, width), jnp.bfloat16),
        grid=(1,),
        in_specs=[ANY, ANY, ANY],
        out_specs=pl.BlockSpec((tok, width), lambda i: (0, 0)),
        scratch_shapes=[
            pltpu.VMEM((tok, 2 * depth), jnp.bfloat16),
            pltpu.VMEM((depth, width), jnp.bfloat16),
            pltpu.VMEM((depth, width), jnp.bfloat16),
            pltpu.SemaphoreType.DMA((width // tile, 2)),
            pltpu.SemaphoreType.DMA,
        ],
        compiler_params=pltpu.CompilerParams(vmem_limit_bytes=64 * 1024 * 1024),
        name="guest_product",
    )(rows, near, far)


def turn(head, cosine, sine):
    return head * cosine + pltpu.roll(head, HD // 2, 1) * sine


def copy_in(sources, targets, sems):
    copies = [
        pltpu.make_async_copy(source, target, sems.at[i])
        for i, (source, target) in enumerate(zip(sources, targets))
    ]
    for copy in copies:
        copy.start()
    return copies


def kv_kernel(count, cos_ref, sin_ref, own_ref, *refs):
    got_hbm, out_ref, got, sems = refs[:count], refs[count], refs[count + 1], refs[count + 2]
    copies = copy_in(got_hbm, [got.at[i] for i in range(count)], sems)
    total = own_ref[...]
    for i, copy in enumerate(copies):
        copy.wait()
        total += got[i].astype(jnp.float32)
    for head in range(KVH):
        cut = slice(head * HD, (head + 1) * HD)
        out_ref[:, cut] = turn(total[:, cut], cos_ref[...], sin_ref[...]).astype(jnp.bfloat16)
    out_ref[:, KW:] = total[:, KW:].astype(jnp.bfloat16)


def finish_kv(own, got, cosine, sine, part):
    step = got[0].shape[0]
    width = 2 * KW
    rows = lambda i: (part, 0)
    return pl.pallas_call(
        functools.partial(kv_kernel, len(got)),
        out_shape=jax.ShapeDtypeStruct((step, width), jnp.bfloat16),
        grid=(1,),
        in_specs=[pl.BlockSpec((step, HD), rows), pl.BlockSpec((step, HD), rows)]
        + [pl.BlockSpec((step, width), lambda i: (part, QW // width))]
        + [ANY] * len(got),
        out_specs=pl.BlockSpec((step, width), lambda i: (0, 0)),
        scratch_shapes=[
            pltpu.VMEM((len(got), step, width), jnp.bfloat16),
            pltpu.SemaphoreType.DMA((len(got),)),
        ],
        compiler_params=pltpu.CompilerParams(vmem_limit_bytes=64 * 1024 * 1024),
        name="finish_kv",
    )(cosine, sine, own, *got)


def attend_kernel(parts, picks, cos_ref, sin_ref, bias_ref, own_ref, *refs):
    blocks = len(picks)
    sources = refs[: parts + blocks]
    out_ref, got, kv, sems = refs[-4:]
    step = got.shape[1]
    targets = [got.at[i] for i in range(parts)]
    targets += [kv.at[pl.ds(i * step, step)] for i in range(blocks)]
    copies = copy_in(sources, targets, sems)
    bias = jnp.concatenate([bias_ref[:, p * step : (p + 1) * step] for p in picks], axis=1)
    for copy in copies:
        copy.wait()
    for group in range(KVH):
        keys = kv[:, group * HD : (group + 1) * HD]
        values = kv[:, KW + group * HD : KW + (group + 1) * HD]
        values = jnp.concatenate([values, jnp.ones_like(values)], axis=1)
        for head in range(group * SHARE, (group + 1) * SHARE):
            cut = slice(head * HD, (head + 1) * HD)
            query = own_ref[:, cut]
            for i in range(parts):
                query += got[i, :, cut].astype(jnp.float32)
            query = turn(query, cos_ref[...], sin_ref[...]).astype(jnp.bfloat16)
            scores = lax.dot_general(
                query, keys, (((1,), (1,)), ((), ())), preferred_element_type=jnp.float32
            )
            scores = scores + bias
            peak = jnp.max(scores, axis=-1, keepdims=True)
            expo = jnp.exp2((scores - peak) * EXP2_SCALE).astype(jnp.bfloat16)
            sums = jnp.dot(expo, values, preferred_element_type=jnp.float32)
            out_ref[:, cut] = (sums[:, :HD] / sums[:, HD:]).astype(jnp.bfloat16)


def attend(own, got, kv_blocks, picks, bias, cosine, sine, part, previous):
    tok = own.shape[0]
    step = tok // HALVES
    blocks = len(picks)
    rows = lambda i: (part, 0)
    in_specs = [
        pl.BlockSpec((step, HD), rows),
        pl.BlockSpec((step, HD), rows),
        pl.BlockSpec((step, bias.shape[1]), rows),
        pl.BlockSpec((step, QW), rows),
    ]
    in_specs += [ANY] * (len(got) + blocks)
    operands = [cosine, sine, bias, own, *got, *kv_blocks]
    aliases = {}
    if previous is not None:
        aliases = {len(operands): 0}
        operands.append(previous)
        in_specs.append(ANY)
    return pl.pallas_call(
        functools.partial(attend_kernel, len(got), picks),
        out_shape=jax.ShapeDtypeStruct((tok, QW), jnp.bfloat16),
        grid=(1,),
        in_specs=in_specs,
        out_specs=pl.BlockSpec((step, QW), rows),
        scratch_shapes=[
            pltpu.VMEM((len(got), step, QW), jnp.bfloat16),
            pltpu.VMEM((blocks * step, 2 * KW), jnp.bfloat16),
            pltpu.SemaphoreType.DMA((len(got) + blocks,)),
        ],
        input_output_aliases=aliases,
        compiler_params=pltpu.CompilerParams(vmem_limit_bytes=64 * 1024 * 1024),
        name="attend",
    )(*operands)


def local(tokens, norm_gain, qkv_weight, doc_ids):
    count = lax.axis_size("seq")
    rank = lax.axis_index("seq")
    ranks = lax.axis_size("dp")
    chips = ranks // 2
    tok = tokens.shape[1]
    depth = qkv_weight.shape[0]
    step = tok // HALVES
    reach = tok * count // 2 - 1
    hops = -(-reach // tok)

    def away(part, j):
        return lax.ppermute(part, "dp", [(i, (i + 2 * j) % ranks) for i in range(ranks)])

    def home(part, j):
        return lax.ppermute(part, "dp", [(i, (i - 2 * j) % ranks) for i in range(ranks)])

    near = qkv_weight
    far = lax.ppermute(qkv_weight, "dp", [(i, i ^ 1) for i in range(ranks)])
    gain = norm_gain
    guests = []
    rows = tokens[0]
    for part in range(HALVES):
        sent = norm_sent(rows, gain, part, depth, chips)
        guests.append([away(piece, j) for j, piece in enumerate(sent, 1)])

    half = HD // 2
    places = (rank * tok + jnp.arange(tok, dtype=jnp.int32)).astype(jnp.float32)
    freqs = 500000.0 ** (-2.0 * jnp.arange(half, dtype=jnp.float32) / HD)
    angles = places[:, None] * freqs[None, :]
    cosine = jnp.cos(angles)
    sine = jnp.sin(angles)
    cosine = jnp.concatenate([cosine, cosine], axis=1)
    sine = jnp.concatenate([-sine, sine], axis=1)

    docs = doc_ids[0]
    spots = jnp.arange(tok, dtype=jnp.int32)
    allow = [(spots[None, :] <= spots[:, None]) & (docs[None, :] == docs[:, None])]
    for hop in range(1, hops + 1):
        other = lax.ppermute(doc_ids, "seq", [(i, i + hop) for i in range(count - hop)])[0]
        allow.append((rank >= hop) & (other[None, :] == docs[:, None]))
    bias = jnp.where(jnp.concatenate(allow, axis=1), 0.0, -1e30).astype(jnp.float32)

    rows, bias, cosine, sine = lax.optimization_barrier((rows, bias, cosine, sine))
    own = own_product(rows, gain, near, far)

    kv_got, q_got = [], []
    for part in range(HALVES):
        sent = [guest_product(piece, near, far, QW, 2 * KW) for piece in guests[part]]
        kv_got.append([home(piece, j) for j, piece in enumerate(sent, 1)])
        sent = [guest_product(piece, near, far, 0, QW) for piece in guests[part]]
        q_got.append([home(piece, j) for j, piece in enumerate(sent, 1)])
    chunks = []
    for part in range(HALVES):
        chunks.append(finish_kv(own, kv_got[part], cosine, sine, part))
    kv_blocks = list(chunks)
    for _ in range(hops):
        for part in range(HALVES):
            chunks[part] = lax.ppermute(chunks[part], "seq", [(i, i + 1) for i in range(count - 1)])
        kv_blocks += chunks

    result = None
    for part in range(HALVES):
        picks = []
        for p in range(len(kv_blocks)):
            start = -(p // HALVES) * tok + (p % HALVES) * step
            ahead = start > (part + 1) * step - 1
            behind = part * step - (start + step - 1) > reach
            if not (ahead or behind):
                picks.append(p)
        result = attend(
            own,
            q_got[part],
            [kv_blocks[p] for p in picks],
            picks,
            bias,
            cosine,
            sine,
            part,
            result,
        )
    return result[None]


def solution(mesh):
    in_specs = (P(("group", "dp"), "seq", None), P(), P("dp", None), P(("group", "dp"), "seq"))
    out_specs = P(("group", "dp"), "seq", None)
    return jax.shard_map(local, mesh=mesh, in_specs=in_specs, out_specs=out_specs, check_vma=False)
```

```python
import functools
import math

import jax
import jax.numpy as jnp
from jax import lax
from jax.experimental import pallas as pl
from jax.experimental.pallas import tpu as pltpu
from jax.sharding import PartitionSpec as P


HD = 128
QH = 16
KVH = 4
QW = 2048
KW = 512
SHARE = QH // KVH
EXP2_SCALE = math.log2(math.e) / math.sqrt(HD)
HALVES = 2

ANY = pl.BlockSpec(memory_space=pl.ANY)
VMEM = pl.BlockSpec(memory_space=pltpu.VMEM)
PARAMS = pltpu.CompilerParams(vmem_limit_bytes=20 * 1024 * 1024)


def row_scale(values):
    return lax.rsqrt(jnp.mean(values * values, axis=-1, keepdims=True) + 1e-05)


def write_blocks(tok_ref, gain_ref, scale, out_ref, chip, core):
    depth = out_ref.shape[1] // 2
    for half in range(2):
        block = 2 * chip + (core if half == 0 else 1 - core)
        cut = pl.ds(pl.multiple_of(block * depth, 128), depth)
        piece = tok_ref[:, cut].astype(jnp.float32) * scale
        piece = piece * gain_ref[cut].astype(jnp.float32)[None, :]
        out_ref[:, half * depth : (half + 1) * depth] = piece.astype(jnp.bfloat16)


def norm_kernel(chips, part, tok_ref, gain_ref, *out_refs):
    place = lax.axis_index("dp")
    step = out_refs[0].shape[0]
    tok_ref = tok_ref.at[pl.ds(part * step, step)]
    scale = row_scale(tok_ref[...].astype(jnp.float32))
    for j, out_ref in enumerate(out_refs, 1):
        chip = lax.rem(lax.div(place, 2) + j, chips)
        write_blocks(tok_ref, gain_ref, scale, out_ref, chip, lax.rem(place, 2))


def norm_sent(rows, gain, part, depth, chips):
    step = rows.shape[0] // HALVES
    return pl.pallas_call(
        functools.partial(norm_kernel, chips, part),
        out_shape=[jax.ShapeDtypeStruct((step, 2 * depth), jnp.bfloat16)] * (chips - 1),
        in_specs=[VMEM, VMEM],
        out_specs=[VMEM] * (chips - 1),
        compiler_params=PARAMS,
        name="norm_sent",
    )(rows, gain)


def multiply(rows, near, far, first, out_ref, tile=512):
    depth = near.shape[0]
    for start in range(0, out_ref.shape[1], tile):
        cut = slice(first + start, first + start + tile)
        total = jnp.dot(rows[:, :depth], near[:, cut], preferred_element_type=jnp.float32)
        total += jnp.dot(rows[:, depth:], far[:, cut], preferred_element_type=jnp.float32)
        out_ref[:, start : start + tile] = total.astype(out_ref.dtype)


def own_kernel(tok_ref, gain_ref, near, far, out_ref, mine):
    place = lax.axis_index("dp")
    scale = row_scale(tok_ref[...].astype(jnp.float32))
    write_blocks(tok_ref, gain_ref, scale, mine, lax.div(place, 2), lax.rem(place, 2))
    multiply(mine, near, far, 0, out_ref)


def own_product(rows, gain, near, far):
    tok = rows.shape[0]
    depth, columns = near.shape
    return pl.pallas_call(
        own_kernel,
        out_shape=jax.ShapeDtypeStruct((tok, columns), jnp.float32),
        in_specs=[VMEM] * 4,
        out_specs=VMEM,
        scratch_shapes=[pltpu.VMEM((tok, 2 * depth), jnp.bfloat16)],
        compiler_params=PARAMS,
        name="own_product",
    )(rows, gain, near, far)


def guest_kernel(first, rows, near, far, out_ref):
    multiply(rows, near, far, first, out_ref)


def guest_product(rows, near, far, first, width):
    return pl.pallas_call(
        functools.partial(guest_kernel, first),
        out_shape=jax.ShapeDtypeStruct((rows.shape[0], width), jnp.bfloat16),
        in_specs=[VMEM] * 3,
        out_specs=VMEM,
        compiler_params=PARAMS,
        name="guest_product",
    )(rows, near, far)


def turn(head, cosine, sine):
    return head * cosine + pltpu.roll(head, HD // 2, 1) * sine


def kv_kernel(part, cos_ref, sin_ref, own_ref, *refs):
    *got_refs, out_ref = refs
    step = out_ref.shape[0]
    rows = slice(part * step, (part + 1) * step)
    cosine, sine = cos_ref[rows], sin_ref[rows]
    for start in range(0, 2 * KW, HD):
        cut = slice(start, start + HD)
        total = own_ref[rows, QW + start : QW + start + HD]
        for got_ref in got_refs:
            total += got_ref[:, cut].astype(jnp.float32)
        if start < KW:
            total = turn(total, cosine, sine)
        out_ref[:, cut] = total.astype(jnp.bfloat16)


def finish_kv(own, got, cosine, sine, part):
    return pl.pallas_call(
        functools.partial(kv_kernel, part),
        out_shape=jax.ShapeDtypeStruct(got[0].shape, jnp.bfloat16),
        in_specs=[VMEM] * (3 + len(got)),
        out_specs=VMEM,
        compiler_params=PARAMS,
        name="finish_kv",
    )(cosine, sine, own, *got)


def attend_kernel(part, parts, picks, cos_ref, sin_ref, bias_ref, own_ref, *refs):
    blocks = len(picks)
    got_refs = refs[:parts]
    kv_refs = refs[parts : parts + blocks]
    out_hbm, out, sems = refs[-3:]
    step = out.shape[0]
    rows = slice(part * step, (part + 1) * step)
    cosine, sine = cos_ref[rows], sin_ref[rows]
    bias = jnp.concatenate([bias_ref[rows, p * step : (p + 1) * step] for p in picks], axis=1)
    copies = []
    for group in range(KVH):
        start = group * HD
        keys = jnp.concatenate([ref[:, start : start + HD] for ref in kv_refs], axis=0)
        start += KW
        values = jnp.concatenate([ref[:, start : start + HD] for ref in kv_refs], axis=0)
        values = jnp.concatenate([values, jnp.ones_like(values)], axis=1)
        for head in range(group * SHARE, (group + 1) * SHARE):
            cut = slice(head * HD, (head + 1) * HD)
            query = own_ref[rows, cut]
            for got_ref in got_refs:
                query += got_ref[:, cut].astype(jnp.float32)
            query = turn(query, cosine, sine).astype(jnp.bfloat16)
            scores = lax.dot_general(
                query, keys, (((1,), (1,)), ((), ())), preferred_element_type=jnp.float32
            )
            scores = scores + bias
            peak = jnp.max(scores, axis=-1, keepdims=True)
            expo = jnp.exp2((scores - peak) * EXP2_SCALE).astype(jnp.bfloat16)
            sums = jnp.dot(expo, values, preferred_element_type=jnp.float32)
            out[:, cut] = (sums[:, :HD] / sums[:, HD:]).astype(jnp.bfloat16)
        cut = pl.ds(group * SHARE * HD, SHARE * HD)
        copy = pltpu.make_async_copy(
            out.at[:, cut], out_hbm.at[pl.ds(part * step, step), cut], sems.at[group]
        )
        copy.start()
        copies.append(copy)
    for copy in copies:
        copy.wait()


def attend(own, got, kv_blocks, picks, bias, cosine, sine, part, previous):
    tok = own.shape[0]
    step = tok // HALVES
    operands = [cosine, sine, bias, own, *got, *kv_blocks]
    in_specs = [VMEM] * len(operands)
    aliases = {}
    if previous is not None:
        aliases = {len(operands): 0}
        operands.append(previous)
        in_specs.append(ANY)
    return pl.pallas_call(
        functools.partial(attend_kernel, part, len(got), picks),
        out_shape=jax.ShapeDtypeStruct((tok, QW), jnp.bfloat16),
        in_specs=in_specs,
        out_specs=ANY,
        scratch_shapes=[
            pltpu.VMEM((step, QW), jnp.bfloat16),
            pltpu.SemaphoreType.DMA((KVH,)),
        ],
        input_output_aliases=aliases,
        compiler_params=PARAMS,
        name="attend",
    )(*operands)


def local(tokens, norm_gain, qkv_weight, doc_ids):
    count = lax.axis_size("seq")
    rank = lax.axis_index("seq")
    ranks = lax.axis_size("dp")
    chips = ranks // 2
    tok = tokens.shape[1]
    depth = qkv_weight.shape[0]
    step = tok // HALVES
    reach = tok * count // 2 - 1
    hops = -(-reach // tok)

    def away(part, j):
        return lax.ppermute(part, "dp", [(i, (i + 2 * j) % ranks) for i in range(ranks)])

    def home(part, j):
        return lax.ppermute(part, "dp", [(i, (i - 2 * j) % ranks) for i in range(ranks)])

    near = qkv_weight
    far = lax.ppermute(qkv_weight, "dp", [(i, i ^ 1) for i in range(ranks)])
    gain = norm_gain
    guests = []
    rows = tokens[0]
    for part in range(HALVES):
        sent = norm_sent(rows, gain, part, depth, chips)
        guests.append([away(piece, j) for j, piece in enumerate(sent, 1)])

    half = HD // 2
    places = (rank * tok + jnp.arange(tok, dtype=jnp.int32)).astype(jnp.float32)
    freqs = 500000.0 ** (-2.0 * jnp.arange(half, dtype=jnp.float32) / HD)
    angles = places[:, None] * freqs[None, :]
    cosine = jnp.cos(angles)
    sine = jnp.sin(angles)
    cosine = jnp.concatenate([cosine, cosine], axis=1)
    sine = jnp.concatenate([-sine, sine], axis=1)

    docs = doc_ids[0]
    spots = jnp.arange(tok, dtype=jnp.int32)
    allow = [(spots[None, :] <= spots[:, None]) & (docs[None, :] == docs[:, None])]
    for hop in range(1, hops + 1):
        other = lax.ppermute(doc_ids, "seq", [(i, i + hop) for i in range(count - hop)])[0]
        allow.append((rank >= hop) & (other[None, :] == docs[:, None]))
    bias = jnp.where(jnp.concatenate(allow, axis=1), 0.0, -1e30).astype(jnp.float32)

    guests[1], bias, cosine, sine = lax.optimization_barrier((guests[1], bias, cosine, sine))
    own = own_product(rows, gain, near, far)

    kv_got, q_got = [], []
    for part in range(HALVES):
        sent = [guest_product(piece, near, far, QW, 2 * KW) for piece in guests[part]]
        kv_got.append([home(piece, j) for j, piece in enumerate(sent, 1)])
        sent = [guest_product(piece, near, far, 0, QW) for piece in guests[part]]
        q_got.append([home(piece, j) for j, piece in enumerate(sent, 1)])
    chunks = []
    for part in range(HALVES):
        chunks.append(finish_kv(own, kv_got[part], cosine, sine, part))
    kv_blocks = list(chunks)
    for _ in range(hops):
        for part in range(HALVES):
            chunks[part] = lax.ppermute(chunks[part], "seq", [(i, i + 1) for i in range(count - 1)])
        kv_blocks += chunks

    result = None
    for part in range(HALVES):
        picks = []
        for p in range(len(kv_blocks)):
            start = -(p // HALVES) * tok + (p % HALVES) * step
            ahead = start > (part + 1) * step - 1
            behind = part * step - (start + step - 1) > reach
            if not (ahead or behind):
                picks.append(p)
        result = attend(
            own,
            q_got[part],
            [kv_blocks[p] for p in picks],
            picks,
            bias,
            cosine,
            sine,
            part,
            result,
        )
    return result[None]


def solution(mesh):
    in_specs = (P(("group", "dp"), "seq", None), P(), P("dp", None), P(("group", "dp"), "seq"))
    out_specs = P(("group", "dp"), "seq", None)
    return jax.shard_map(local, mesh=mesh, in_specs=in_specs, out_specs=out_specs, check_vma=False)
```

```python
import functools
import math

import jax
import jax.numpy as jnp
from jax import lax
from jax.experimental import pallas as pl
from jax.experimental.pallas import tpu as pltpu
from jax.sharding import PartitionSpec as P


HD = 128
QH = 16
KVH = 4
QW = 2048
KW = 512
SHARE = QH // KVH
EXP2_SCALE = math.log2(math.e) / math.sqrt(HD)
HALVES = 2

ANY = pl.BlockSpec(memory_space=pl.ANY)
VMEM = pl.BlockSpec(memory_space=pltpu.VMEM)
PARAMS = pltpu.CompilerParams(vmem_limit_bytes=20 * 1024 * 1024)


def row_scale(values):
    return lax.rsqrt(jnp.mean(values * values, axis=-1, keepdims=True) + 1e-05)


def write_blocks(tok_ref, gain_ref, scale, out_ref, chip, core):
    depth = out_ref.shape[1] // 2
    for half in range(2):
        block = 2 * chip + (core if half == 0 else 1 - core)
        cut = pl.ds(pl.multiple_of(block * depth, 128), depth)
        piece = tok_ref[:, cut].astype(jnp.float32) * scale
        piece = piece * gain_ref[cut].astype(jnp.float32)[None, :]
        out_ref[:, half * depth : (half + 1) * depth] = piece.astype(jnp.bfloat16)


def norm_kernel(chips, tok_ref, gain_ref, *out_refs):
    place = lax.axis_index("dp")
    scale = row_scale(tok_ref[...].astype(jnp.float32))
    for j, out_ref in enumerate(out_refs, 1):
        chip = lax.rem(lax.div(place, 2) + j, chips)
        write_blocks(tok_ref, gain_ref, scale, out_ref, chip, lax.rem(place, 2))


def norm_sent(rows, gain, part, depth, chips):
    tok, width = rows.shape
    step = tok // HALVES
    return pl.pallas_call(
        functools.partial(norm_kernel, chips),
        out_shape=[jax.ShapeDtypeStruct((step, 2 * depth), jnp.bfloat16)] * (chips - 1),
        grid=(1,),
        in_specs=[
            pl.BlockSpec((step, width), lambda i: (part, 0)),
            pl.BlockSpec((width,), lambda i: (0,)),
        ],
        out_specs=[pl.BlockSpec((step, 2 * depth), lambda i: (0, 0))] * (chips - 1),
        compiler_params=PARAMS,
        name="norm_sent",
    )(rows, gain)


def multiply(rows, near, far, first, out_ref, tile=512):
    depth = near.shape[0]
    for start in range(0, out_ref.shape[1], tile):
        cut = slice(first + start, first + start + tile)
        total = jnp.dot(rows[:, :depth], near[:, cut], preferred_element_type=jnp.float32)
        total += jnp.dot(rows[:, depth:], far[:, cut], preferred_element_type=jnp.float32)
        out_ref[:, start : start + tile] = total.astype(out_ref.dtype)


def own_kernel(
    tok_hbm, gain_hbm, near_hbm, far_hbm, out_ref, near, far, tok_ref, gain_ref, mine, sems
):
    tile = 512
    _, columns = near.shape
    tok_copy = pltpu.make_async_copy(tok_hbm, tok_ref, sems.at[0, columns // tile])
    tok_copy.start()
    gain_copy = pltpu.make_async_copy(gain_hbm, gain_ref, sems.at[1, columns // tile])
    gain_copy.start()
    copies = []
    for start in range(0, columns, tile):
        cut = pl.ds(start, tile)
        for i, (source, target) in enumerate(((near_hbm, near), (far_hbm, far))):
            copy = pltpu.make_async_copy(
                source.at[:, cut], target.at[:, cut], sems.at[i, start // tile]
            )
            copy.start()
            copies.append(copy)
    place = lax.axis_index("dp")
    tok_copy.wait()
    gain_copy.wait()
    scale = row_scale(tok_ref[...].astype(jnp.float32))
    write_blocks(tok_ref, gain_ref, scale, mine, lax.div(place, 2), lax.rem(place, 2))
    for start in range(0, columns, tile):
        copies[2 * start // tile].wait()
        copies[2 * start // tile + 1].wait()
        multiply(mine, near, far, start, out_ref.at[:, pl.ds(start, tile)])


def own_product(rows, gain, near, far):
    tok, width = rows.shape
    depth, columns = near.shape
    kept = jax.ShapeDtypeStruct(near.shape, near.dtype)
    return pl.pallas_call(
        own_kernel,
        out_shape=[jax.ShapeDtypeStruct((tok, columns), jnp.float32), kept, kept],
        in_specs=[ANY, ANY, ANY, ANY],
        out_specs=[VMEM] * 3,
        scratch_shapes=[
            pltpu.VMEM((tok, width), jnp.bfloat16),
            pltpu.VMEM((width,), jnp.bfloat16),
            pltpu.VMEM((tok, 2 * depth), jnp.bfloat16),
            pltpu.SemaphoreType.DMA((2, columns // 512 + 1)),
        ],
        compiler_params=PARAMS,
        name="own_product",
    )(rows, gain, near, far)


def guest_kernel(first, rows, near, far, out_ref):
    multiply(rows, near, far, first, out_ref)


def guest_product(rows, near, far, first, width):
    return pl.pallas_call(
        functools.partial(guest_kernel, first),
        out_shape=jax.ShapeDtypeStruct((rows.shape[0], width), jnp.bfloat16),
        in_specs=[VMEM] * 3,
        out_specs=VMEM,
        compiler_params=PARAMS,
        name="guest_product",
    )(rows, near, far)


def turn(head, cosine, sine):
    return head * cosine + pltpu.roll(head, HD // 2, 1) * sine


def kv_kernel(part, cos_ref, sin_ref, own_ref, *refs):
    *got_refs, out_ref = refs
    step = out_ref.shape[0]
    rows = slice(part * step, (part + 1) * step)
    cosine, sine = cos_ref[rows], sin_ref[rows]
    for start in range(0, 2 * KW, HD):
        cut = slice(start, start + HD)
        total = own_ref[rows, QW + start : QW + start + HD]
        for got_ref in got_refs:
            total += got_ref[:, cut].astype(jnp.float32)
        if start < KW:
            total = turn(total, cosine, sine)
        out_ref[:, cut] = total.astype(jnp.bfloat16)


def finish_kv(own, got, cosine, sine, part):
    return pl.pallas_call(
        functools.partial(kv_kernel, part),
        out_shape=jax.ShapeDtypeStruct(got[0].shape, jnp.bfloat16),
        in_specs=[VMEM] * (3 + len(got)),
        out_specs=VMEM,
        compiler_params=PARAMS,
        name="finish_kv",
    )(cosine, sine, own, *got)


def attend_kernel(part, parts, picks, cos_ref, sin_ref, bias_ref, own_ref, *refs):
    blocks = len(picks)
    got_refs = refs[:parts]
    kv_refs = refs[parts : parts + blocks]
    out_hbm, out, sems = refs[-3:]
    step = out.shape[0]
    rows = slice(part * step, (part + 1) * step)
    cosine, sine = cos_ref[rows], sin_ref[rows]
    bias = jnp.concatenate([bias_ref[rows, p * step : (p + 1) * step] for p in picks], axis=1)
    copies = []
    for group in range(KVH):
        start = group * HD
        keys = jnp.concatenate([ref[:, start : start + HD] for ref in kv_refs], axis=0)
        start += KW
        values = jnp.concatenate([ref[:, start : start + HD] for ref in kv_refs], axis=0)
        values = jnp.concatenate([values, jnp.ones_like(values)], axis=1)
        for head in range(group * SHARE, (group + 1) * SHARE):
            cut = slice(head * HD, (head + 1) * HD)
            query = own_ref[rows, cut]
            for got_ref in got_refs:
                query += got_ref[:, cut].astype(jnp.float32)
            query = turn(query, cosine, sine).astype(jnp.bfloat16)
            scores = lax.dot_general(
                query, keys, (((1,), (1,)), ((), ())), preferred_element_type=jnp.float32
            )
            scores = scores + bias
            peak = jnp.max(scores, axis=-1, keepdims=True)
            expo = jnp.exp2((scores - peak) * EXP2_SCALE).astype(jnp.bfloat16)
            sums = jnp.dot(expo, values, preferred_element_type=jnp.float32)
            out[:, cut] = (sums[:, :HD] / sums[:, HD:]).astype(jnp.bfloat16)
        cut = pl.ds(group * SHARE * HD, SHARE * HD)
        copy = pltpu.make_async_copy(
            out.at[:, cut], out_hbm.at[pl.ds(part * step, step), cut], sems.at[group]
        )
        copy.start()
        copies.append(copy)
    for copy in copies:
        copy.wait()


def attend(own, got, kv_blocks, picks, bias, cosine, sine, part, previous):
    tok = own.shape[0]
    step = tok // HALVES
    operands = [cosine, sine, bias, own, *got, *kv_blocks]
    in_specs = [VMEM] * len(operands)
    aliases = {}
    if previous is not None:
        aliases = {len(operands): 0}
        operands.append(previous)
        in_specs.append(ANY)
    return pl.pallas_call(
        functools.partial(attend_kernel, part, len(got), picks),
        out_shape=jax.ShapeDtypeStruct((tok, QW), jnp.bfloat16),
        in_specs=in_specs,
        out_specs=ANY,
        scratch_shapes=[
            pltpu.VMEM((step, QW), jnp.bfloat16),
            pltpu.SemaphoreType.DMA((KVH,)),
        ],
        input_output_aliases=aliases,
        compiler_params=PARAMS,
        name="attend",
    )(*operands)


def local(tokens, norm_gain, qkv_weight, doc_ids):
    count = lax.axis_size("seq")
    rank = lax.axis_index("seq")
    ranks = lax.axis_size("dp")
    chips = ranks // 2
    tok = tokens.shape[1]
    depth = qkv_weight.shape[0]
    step = tok // HALVES
    reach = tok * count // 2 - 1
    hops = -(-reach // tok)

    def away(part, j):
        return lax.ppermute(part, "dp", [(i, (i + 2 * j) % ranks) for i in range(ranks)])

    def home(part, j):
        return lax.ppermute(part, "dp", [(i, (i - 2 * j) % ranks) for i in range(ranks)])

    near = qkv_weight
    far = lax.ppermute(qkv_weight, "dp", [(i, i ^ 1) for i in range(ranks)])
    gain = pltpu.with_memory_space_constraint(norm_gain, pltpu.HBM)
    rows = pltpu.with_memory_space_constraint(tokens[0], pltpu.HBM)
    guests = []
    for part in range(HALVES):
        sent = norm_sent(rows, gain, part, depth, chips)
        guests.append([away(piece, j) for j, piece in enumerate(sent, 1)])

    half = HD // 2
    places = (rank * tok + jnp.arange(tok, dtype=jnp.int32)).astype(jnp.float32)
    freqs = 500000.0 ** (-2.0 * jnp.arange(half, dtype=jnp.float32) / HD)
    angles = places[:, None] * freqs[None, :]
    cosine = jnp.cos(angles)
    sine = jnp.sin(angles)
    cosine = jnp.concatenate([cosine, cosine], axis=1)
    sine = jnp.concatenate([-sine, sine], axis=1)

    docs = doc_ids[0]
    spots = jnp.arange(tok, dtype=jnp.int32)
    allow = [(spots[None, :] <= spots[:, None]) & (docs[None, :] == docs[:, None])]
    for hop in range(1, hops + 1):
        other = lax.ppermute(doc_ids, "seq", [(i, i + hop) for i in range(count - hop)])[0]
        allow.append((rank >= hop) & (other[None, :] == docs[:, None]))
    bias = jnp.where(jnp.concatenate(allow, axis=1), 0.0, -1e30).astype(jnp.float32)

    near = pltpu.with_memory_space_constraint(near, pltpu.HBM)
    own, near, far = own_product(rows, gain, near, far)

    kv_got, q_got = [], []
    for part in range(HALVES):
        sent = [guest_product(piece, near, far, QW, 2 * KW) for piece in guests[part]]
        kv_got.append([home(piece, j) for j, piece in enumerate(sent, 1)])
        sent = [guest_product(piece, near, far, 0, QW) for piece in guests[part]]
        q_got.append([home(piece, j) for j, piece in enumerate(sent, 1)])
    chunks = []
    for part in range(HALVES):
        chunks.append(finish_kv(own, kv_got[part], cosine, sine, part))
    kv_blocks = list(chunks)
    for _ in range(hops):
        for part in range(HALVES):
            chunks[part] = lax.ppermute(chunks[part], "seq", [(i, i + 1) for i in range(count - 1)])
        kv_blocks += chunks

    result = None
    for part in range(HALVES):
        picks = []
        for p in range(len(kv_blocks)):
            start = -(p // HALVES) * tok + (p % HALVES) * step
            ahead = start > (part + 1) * step - 1
            behind = part * step - (start + step - 1) > reach
            if not (ahead or behind):
                picks.append(p)
        result = attend(
            own,
            q_got[part],
            [kv_blocks[p] for p in picks],
            picks,
            bias,
            cosine,
            sine,
            part,
            result,
        )
    return result[None]


def solution(mesh):
    in_specs = (P(("group", "dp"), "seq", None), P(), P("dp", None), P(("group", "dp"), "seq"))
    out_specs = P(("group", "dp"), "seq", None)
    return jax.shard_map(local, mesh=mesh, in_specs=in_specs, out_specs=out_specs, check_vma=False)
```
